128 devices in a mesh: row: 8 (over z, core), col: 16 (over x, y).
Axes of the slice: x: 4, y: 4, z: 4, core: 2. Of those that a mesh axis runs over, the one named last changes fastest.
Arguments:
- features: bfloat16 [262144, 256], P(('row', 'col')), may hold values from -6 to 6
- send_rows: int32 [2048, 256], P(('row', 'col')), may hold values from 0 to 2047
- send_count: int32 [2048], P(('row', 'col')), may hold values from 129 to 256, as said below
- hub_rows: int32 [4096], P(('row', 'col')), may hold values from 0 to 2047
- neighbours: int32 [262144, 16], P(('row', 'col')), may hold values from 0 to 10239
- w_self: bfloat16 [256, 256], replicated, may hold values from -0.375 to 0.375
- w_neigh: bfloat16 [256, 256], replicated, may hold values from -0.375 to 0.375
- bias_vector: float32 [256], replicated, may hold values from -3 to 3
- cotangent: bfloat16 [262144, 256], P(('row', 'col')), may hold values from -6 to 6
Outputs:
- output_rows: bfloat16 [262144, 256], P(('row', 'col'))
- feature_grads: float32 [262144, 256], P(('row', 'col'))
The draws below stay inside these ranges and needn't reach their ends.
Inputs may be any that keep to these rules, and one draw needn't show every extreme that they name: `send_count`: on every device, at least one of its 16 halo lists has its full length 256.
All inputs are finite; a program needn't handle non-finite values.
Results may differ from the reference program's by a relative error of at most 0.003.
Values may be sent and summed in bfloat16 or wider, within the bound.
A program may use at most 128 MiB of HBM per device.

```python
import jax
import jax.numpy as jnp
from jax import lax

D = 256
DEG = 16
V_DEV = 2048
C = 256
HUB_DEV = 32
HUBS = 4096
VERTS = 262144
SRC = 10240
N_ROW = 8
N_COL = 16


def draw_send_count(key, part):
    first_key, second_key = jax.random.split(jax.random.fold_in(key, 17))
    counts = jax.random.randint(first_key, (N_ROW * N_COL, N_COL), C // 2 + 1, C + 1)
    position = jax.random.randint(second_key, (N_ROW * N_COL, 1), 0, N_COL)
    counts = jnp.where(jnp.arange(N_COL)[None, :] == position, C, counts)
    return counts.reshape(-1).astype(jnp.int32)


def with_ends(result, own_key, smallest, largest):
    longest = result.shape.index(max(result.shape))
    spots = []
    for shift in (0, 1):
        where = [jax.random.randint(jax.random.fold_in(own_key, axis), (), 0, length) for axis, length in enumerate(result.shape)]
        where[longest] = (where[longest] + shift) % result.shape[longest]
        spots.append(tuple(where))
    return result.at[spots[0]].set(smallest).at[spots[1]].set(largest)


def block_scale(stream_key, extent, cuts, smallest, largest):
    level, own = 1.0, jax.random.fold_in(stream_key, 6)
    for dim, blocks in cuts:
        heights = jnp.exp(jax.random.uniform(jax.random.fold_in(own, dim), (blocks,), jnp.float32, smallest / len(cuts), largest / len(cuts)))
        level = level * jnp.repeat(heights, extent[dim] // blocks).reshape([-1 if axis == dim else 1 for axis in range(len(extent))])
    return level


def scatter_about(own_key, dims, deviation, limit, shards=(), kind=jnp.bfloat16):
    factor_of = block_scale(own_key, dims, shards, -0.22, 0.18) if shards else 1.0
    array = jax.random.normal(own_key, dims, jnp.float32) * deviation * factor_of
    return jnp.minimum(jnp.maximum(array, -limit), limit).astype(kind)


def setup_inputs(seed: int = 0) -> dict:
    streams_of = jax.random.split(jax.random.key(seed), 10)
    features = scatter_about(streams_of[0], (VERTS, D), 1.0, 6.0, ((0, 128),))
    send_rows = with_ends(jax.random.randint(streams_of[1], (VERTS // V_DEV * N_COL, C), 0, V_DEV), jax.random.fold_in(streams_of[1], 1), 0, V_DEV - 1).astype(jnp.int32)
    send_count = draw_send_count(jax.random.fold_in(streams_of[9], 71), 0)
    hub_rows = with_ends(jax.random.randint(streams_of[3], (HUBS,), 0, V_DEV), jax.random.fold_in(streams_of[3], 1), 0, V_DEV - 1).astype(jnp.int32)
    neighbours = with_ends(jax.random.randint(streams_of[4], (VERTS, DEG), 0, SRC), jax.random.fold_in(streams_of[4], 1), 0, SRC - 1).astype(jnp.int32)
    w_self = scatter_about(streams_of[5], (D, D), D ** -0.5, 0.375)
    w_neigh = scatter_about(streams_of[6], (D, D), D ** -0.5, 0.375)
    bias_vector = scatter_about(streams_of[7], (D,), 0.5, 3.0, (), jnp.float32)
    cotangent = scatter_about(streams_of[8], (VERTS, D), 1.0, 6.0, ((0, 128),))
    return {"features": features, "send_rows": send_rows, "send_count": send_count, "hub_rows": hub_rows, "neighbours": neighbours, "w_self": w_self, "w_neigh": w_neigh, "bias_vector": bias_vector, "cotangent": cotangent}


def smooth_gate(values):
    return jax.nn.gelu(values, approximate=True)

def device_pass(vertex_rows, source_table, neighbour_rows, cot_rows, w_self, w_neigh, bias_vector):
    gathered = lax.optimization_barrier(jnp.sum(source_table[neighbour_rows].astype(jnp.float32), axis=1))
    aggregated = (gathered * (1.0 / DEG)).astype(jnp.bfloat16)
    preact = jnp.dot(vertex_rows, w_self, preferred_element_type=jnp.float32)
    preact = preact + jnp.dot(aggregated, w_neigh, preferred_element_type=jnp.float32) + bias_vector
    output_rows = smooth_gate(preact).astype(jnp.bfloat16)
    unused, backward = jax.vjp(smooth_gate, preact)
    grad_preact = backward(cot_rows.astype(jnp.float32))[0].astype(jnp.bfloat16)
    grad_direct = jnp.dot(grad_preact, w_self.T, preferred_element_type=jnp.float32)
    grad_aggregated = jnp.dot(grad_preact, w_neigh.T, preferred_element_type=jnp.float32).astype(jnp.bfloat16)
    contrib = jnp.broadcast_to((grad_aggregated.astype(jnp.float32) * (1.0 / DEG))[:, None, :], neighbour_rows.shape + (D,))
    table_grads = jnp.zeros((SRC, D), jnp.float32).at[neighbour_rows.reshape(-1)].add(contrib.reshape(-1, D))
    hub_start = V_DEV + N_COL * C
    return (output_rows, grad_direct + table_grads[:V_DEV], table_grads[V_DEV:hub_start], table_grads[hub_start:])

def pick_rows(vertex_rows, index_rows):
    return vertex_rows[index_rows]

def add_rows(grad_rows, index_rows, values):
    return grad_rows.at[index_rows].add(values)

def reference(features, send_rows, send_count, hub_rows, neighbours, w_self, w_neigh, bias_vector, cotangent):
    device_count = N_ROW * N_COL
    vertex_blocks = features.reshape(N_ROW, N_COL, V_DEV, D)
    send_table = send_rows.reshape(N_ROW, N_COL, N_COL, C)
    live_mask = jnp.arange(C)[None, None, None, :] < send_count.reshape(N_ROW, N_COL, N_COL)[..., None]
    outgoing = jax.vmap(jax.vmap(pick_rows))(vertex_blocks, send_table)
    outgoing = jnp.where(live_mask[..., None], outgoing, jnp.zeros((), outgoing.dtype))
    halos = jnp.swapaxes(outgoing, 1, 2).reshape(device_count, N_COL * C, D)
    hub_index = (jnp.arange(device_count, dtype=jnp.int32)[:, None] * V_DEV + hub_rows.reshape(device_count, HUB_DEV)).reshape(-1)
    hub_table = features[hub_index]

    def one_device(running, inputs):
        vertex_rows, halo_rows, neighbour_rows, cot_rows = inputs
        source_table = jnp.concatenate([vertex_rows, halo_rows, hub_table], axis=0)
        output_rows, grad_rows, halo_grads, hub_grads = device_pass(vertex_rows, source_table, neighbour_rows, cot_rows, w_self, w_neigh, bias_vector)
        return (running + hub_grads, (output_rows, grad_rows, halo_grads))
    hub_sum, stacked = lax.scan(one_device, jnp.zeros((HUBS, D), jnp.float32), (features.reshape(device_count, V_DEV, D), halos, neighbours.reshape(device_count, V_DEV, DEG), cotangent.reshape(device_count, V_DEV, D)))
    output_rows, grad_rows, halo_grads = stacked
    returned = jnp.swapaxes(halo_grads.reshape(N_ROW, N_COL, N_COL, C, D), 1, 2)
    returned = jnp.where(live_mask[..., None], returned, jnp.zeros((), jnp.float32))
    grad_rows = jax.vmap(add_rows)(grad_rows, send_table.reshape(device_count, N_COL * C), returned.reshape(device_count, N_COL * C, D))
    grad_rows = grad_rows.reshape(VERTS, D).at[hub_index].add(hub_sum)
    return (output_rows.reshape(VERTS, D), grad_rows)
```

```python
import jax
import jax.numpy as jnp
from jax import lax
from jax.sharding import PartitionSpec as P


def smooth_gate(values):
    return jax.nn.gelu(values, approximate=True)


def count_matrix(index_rows, start, width):
    degree = index_rows.shape[1]
    column_ids = jnp.arange(start, start + width, dtype=jnp.int32)
    counts = (index_rows[:, 0:1] == column_ids[None, :]).astype(jnp.float32)
    for slot in range(1, degree):
        counts = counts + (index_rows[:, slot : slot + 1] == column_ids[None, :]).astype(
            jnp.float32
        )
    return counts.astype(jnp.bfloat16)


def transposed_dot(counts, values):
    return lax.dot_general(
        counts, values, (((0,), (0,)), ((), ())), preferred_element_type=jnp.float32
    )


def local(
    features, send_rows, send_count, hub_rows, neighbours, w_self, w_neigh, bias_vector, cotangent
):
    vertex_count, feature_width = features.shape
    slot_count = send_rows.shape[1]
    degree = neighbours.shape[1]
    peer_count = lax.axis_size("col")
    hub_count = hub_rows.shape[0]
    device_count = lax.axis_size("row") * peer_count
    halo_width = peer_count * slot_count
    hub_start = vertex_count + halo_width
    live_mask = jnp.arange(slot_count)[None, :] < send_count[:, None]
    outgoing = jnp.where(live_mask[:, :, None], features[send_rows], jnp.zeros((), features.dtype))
    incoming = lax.all_to_all(outgoing, "col", split_axis=0, concat_axis=0, tiled=True)
    incoming = incoming.reshape(-1, feature_width)
    hub_local = features[hub_rows]
    hub_table = lax.all_gather(hub_local, ("row", "col"), axis=0, tiled=True)

    counts_own = count_matrix(neighbours, 0, vertex_count)
    counts_halo = count_matrix(neighbours, vertex_count, halo_width)
    counts_hub = count_matrix(neighbours, hub_start, device_count * hub_count)
    counts_own, counts_halo, counts_hub = lax.optimization_barrier(
        (counts_own, counts_halo, counts_hub)
    )

    summed = jnp.dot(counts_own, features, preferred_element_type=jnp.float32)
    summed = summed + jnp.dot(counts_halo, incoming, preferred_element_type=jnp.float32)
    summed = summed + jnp.dot(counts_hub, hub_table, preferred_element_type=jnp.float32)
    aggregated = (summed * (1.0 / degree)).astype(jnp.bfloat16)
    preact = jnp.dot(features, w_self, preferred_element_type=jnp.float32)
    preact = preact + jnp.dot(aggregated, w_neigh, preferred_element_type=jnp.float32) + bias_vector
    output_rows = smooth_gate(preact).astype(jnp.bfloat16)
    unused, backward = jax.vjp(smooth_gate, preact)
    grad_preact = backward(cotangent.astype(jnp.float32))[0].astype(jnp.bfloat16)
    grad_direct = jnp.dot(grad_preact, w_self.T, preferred_element_type=jnp.float32)
    grad_aggregated = jnp.dot(grad_preact, w_neigh.T, preferred_element_type=jnp.float32).astype(
        jnp.bfloat16
    )
    scaled_grads = (grad_aggregated.astype(jnp.float32) * (1.0 / degree)).astype(jnp.bfloat16)

    hub_back = transposed_dot(counts_hub, scaled_grads)
    hub_parts = lax.all_to_all(
        hub_back.reshape(device_count, hub_count, feature_width),
        ("row", "col"),
        split_axis=0,
        concat_axis=0,
        tiled=True,
    )
    hub_owned = jnp.sum(hub_parts, axis=0)

    halo_back = transposed_dot(counts_halo, scaled_grads)
    returned = lax.all_to_all(
        halo_back.astype(jnp.bfloat16).reshape(peer_count, slot_count, feature_width),
        "col",
        split_axis=0,
        concat_axis=0,
        tiled=True,
    ).astype(jnp.float32)
    returned = jnp.where(live_mask[:, :, None], returned, jnp.zeros((), jnp.float32))
    grad_rows = grad_direct + transposed_dot(counts_own, scaled_grads)
    grad_rows = grad_rows.at[send_rows.reshape(-1)].add(returned.reshape(-1, feature_width))
    grad_rows = grad_rows.at[hub_rows].add(hub_owned)
    return (output_rows, grad_rows)


def solution(mesh):
    return jax.shard_map(
        local,
        mesh=mesh,
        in_specs=(
            P(("row", "col"), None),
            P(("row", "col"), None),
            P(("row", "col")),
            P(("row", "col")),
            P(("row", "col"), None),
            P(),
            P(),
            P(),
            P(("row", "col"), None),
        ),
        out_specs=(P(("row", "col"), None), P(("row", "col"), None)),
        check_vma=False,
    )
```

```python
import jax
import jax.numpy as jnp
from jax import lax
from jax.sharding import PartitionSpec as P


def smooth_gate(values):
    return jax.nn.gelu(values, approximate=True)


def count_matrix(index_rows, start, width):
    degree = index_rows.shape[1]
    column_ids = jnp.arange(start, start + width, dtype=jnp.int32)
    counts = (index_rows[:, 0:1] == column_ids[None, :]).astype(jnp.float32)
    for slot in range(1, degree):
        counts = counts + (index_rows[:, slot : slot + 1] == column_ids[None, :]).astype(
            jnp.float32
        )
    return counts.astype(jnp.bfloat16)


def transposed_dot(counts, values):
    return lax.dot_general(
        counts, values, (((0,), (0,)), ((), ())), preferred_element_type=jnp.float32
    )


def local(
    features, send_rows, send_count, hub_rows, neighbours, w_self, w_neigh, bias_vector, cotangent
):
    vertex_count, feature_width = features.shape
    slot_count = send_rows.shape[1]
    degree = neighbours.shape[1]
    peer_count = lax.axis_size("col")
    hub_count = hub_rows.shape[0]
    device_count = lax.axis_size("row") * peer_count
    halo_width = peer_count * slot_count
    hub_start = vertex_count + halo_width
    live_mask = jnp.arange(slot_count)[None, :] < send_count[:, None]
    row_ids = jnp.arange(vertex_count, dtype=jnp.int32)
    picks = ((send_rows[:, :, None] == row_ids) & live_mask[:, :, None]).astype(features.dtype)
    picks = picks.reshape(halo_width, vertex_count)
    outgoing = jnp.dot(picks, features, preferred_element_type=jnp.float32).astype(features.dtype)
    outgoing = outgoing.reshape(peer_count, slot_count, feature_width)
    incoming = lax.all_to_all(outgoing, "col", split_axis=0, concat_axis=0, tiled=True)
    incoming = incoming.reshape(-1, feature_width)
    hub_local = features[hub_rows]
    hub_table = lax.all_gather(hub_local, ("row", "col"), axis=0, tiled=True)

    counts_own = count_matrix(neighbours, 0, vertex_count)
    counts_halo = count_matrix(neighbours, vertex_count, halo_width)
    counts_hub = count_matrix(neighbours, hub_start, device_count * hub_count)
    counts_own, counts_halo, counts_hub = lax.optimization_barrier(
        (counts_own, counts_halo, counts_hub)
    )

    summed = jnp.dot(counts_own, features, preferred_element_type=jnp.float32)
    summed = summed + jnp.dot(counts_halo, incoming, preferred_element_type=jnp.float32)
    summed = summed + jnp.dot(counts_hub, hub_table, preferred_element_type=jnp.float32)
    aggregated = (summed * (1.0 / degree)).astype(jnp.bfloat16)
    preact = jnp.dot(features, w_self, preferred_element_type=jnp.float32)
    preact = preact + jnp.dot(aggregated, w_neigh, preferred_element_type=jnp.float32) + bias_vector
    output_rows = smooth_gate(preact).astype(jnp.bfloat16)
    unused, backward = jax.vjp(smooth_gate, preact)
    grad_preact = backward(cotangent.astype(jnp.float32))[0].astype(jnp.bfloat16)
    grad_direct = jnp.dot(grad_preact, w_self.T, preferred_element_type=jnp.float32)
    grad_aggregated = jnp.dot(grad_preact, w_neigh.T, preferred_element_type=jnp.float32).astype(
        jnp.bfloat16
    )
    scaled_grads = (grad_aggregated.astype(jnp.float32) * (1.0 / degree)).astype(jnp.bfloat16)

    hub_back = transposed_dot(counts_hub, scaled_grads)
    hub_parts = lax.all_to_all(
        hub_back.reshape(device_count, hub_count, feature_width),
        ("row", "col"),
        split_axis=0,
        concat_axis=0,
        tiled=True,
    )
    hub_owned = jnp.sum(hub_parts, axis=0)

    halo_back = transposed_dot(counts_halo, scaled_grads)
    returned = lax.all_to_all(
        halo_back.astype(jnp.bfloat16).reshape(peer_count, slot_count, feature_width),
        "col",
        split_axis=0,
        concat_axis=0,
        tiled=True,
    )
    grad_rows = grad_direct + transposed_dot(counts_own, scaled_grads)
    grad_rows = grad_rows + transposed_dot(picks, returned.reshape(halo_width, feature_width))
    grad_rows = grad_rows.at[hub_rows].add(hub_owned)
    return (output_rows, grad_rows)


def solution(mesh):
    return jax.shard_map(
        local,
        mesh=mesh,
        in_specs=(
            P(("row", "col"), None),
            P(("row", "col"), None),
            P(("row", "col")),
            P(("row", "col")),
            P(("row", "col"), None),
            P(),
            P(),
            P(),
            P(("row", "col"), None),
        ),
        out_specs=(P(("row", "col"), None), P(("row", "col"), None)),
        check_vma=False,
    )
```

```python
import jax
import jax.numpy as jnp
from jax import lax
from jax.sharding import PartitionSpec as P


def smooth_gate(values):
    return jax.nn.gelu(values, approximate=True)


def count_matrix(index_rows, start, width):
    degree = index_rows.shape[1]
    narrow_rows = index_rows.astype(jnp.int16)
    column_ids = jnp.arange(start, start + width, dtype=jnp.int16)
    counts = (narrow_rows[:, 0:1] == column_ids[None, :]).astype(jnp.bfloat16)
    for slot in range(1, degree):
        counts = counts + (narrow_rows[:, slot : slot + 1] == column_ids[None, :]).astype(
            jnp.bfloat16
        )
    return counts


def transposed_dot(counts, values):
    return lax.dot_general(
        counts, values, (((0,), (0,)), ((), ())), preferred_element_type=jnp.float32
    )


def local(
    features, send_rows, send_count, hub_rows, neighbours, w_self, w_neigh, bias_vector, cotangent
):
    vertex_count, feature_width = features.shape
    slot_count = send_rows.shape[1]
    degree = neighbours.shape[1]
    peer_count = lax.axis_size("col")
    hub_count = hub_rows.shape[0]
    device_count = lax.axis_size("row") * peer_count
    halo_width = peer_count * slot_count
    hub_start = vertex_count + halo_width
    live_mask = jnp.arange(slot_count)[None, :] < send_count[:, None]
    row_ids = jnp.arange(vertex_count, dtype=jnp.int32)
    picks = ((send_rows[:, :, None] == row_ids) & live_mask[:, :, None]).astype(features.dtype)
    picks = picks.reshape(halo_width, vertex_count)
    outgoing = jnp.dot(picks, features, preferred_element_type=jnp.float32).astype(features.dtype)
    outgoing = outgoing.reshape(peer_count, slot_count, feature_width)
    incoming = lax.all_to_all(outgoing, "col", split_axis=0, concat_axis=0, tiled=True)
    incoming = incoming.reshape(-1, feature_width)
    hub_local = features[hub_rows]
    hub_table = lax.all_gather(hub_local, ("row", "col"), axis=0, tiled=True)

    counts_own = count_matrix(neighbours, 0, vertex_count)
    counts_halo = count_matrix(neighbours, vertex_count, halo_width)
    counts_hub = count_matrix(neighbours, hub_start, device_count * hub_count)
    counts_own, counts_halo, counts_hub = lax.optimization_barrier(
        (counts_own, counts_halo, counts_hub)
    )

    summed = jnp.dot(counts_own, features, preferred_element_type=jnp.float32)
    summed = summed + jnp.dot(counts_halo, incoming, preferred_element_type=jnp.float32)
    summed = summed + jnp.dot(counts_hub, hub_table, preferred_element_type=jnp.float32)
    aggregated = (summed * (1.0 / degree)).astype(jnp.bfloat16)
    preact = jnp.dot(features, w_self, preferred_element_type=jnp.float32)
    preact = preact + jnp.dot(aggregated, w_neigh, preferred_element_type=jnp.float32) + bias_vector
    output_rows = smooth_gate(preact).astype(jnp.bfloat16)
    unused, backward = jax.vjp(smooth_gate, preact)
    grad_preact = backward(cotangent.astype(jnp.float32))[0].astype(jnp.bfloat16)
    grad_direct = jnp.dot(grad_preact, w_self.T, preferred_element_type=jnp.float32)
    grad_aggregated = jnp.dot(grad_preact, w_neigh.T, preferred_element_type=jnp.float32).astype(
        jnp.bfloat16
    )
    scaled_grads = (grad_aggregated.astype(jnp.float32) * (1.0 / degree)).astype(jnp.bfloat16)

    hub_back = transposed_dot(counts_hub, scaled_grads)
    hub_parts = lax.all_to_all(
        hub_back.reshape(device_count, hub_count, feature_width),
        ("row", "col"),
        split_axis=0,
        concat_axis=0,
        tiled=True,
    )
    hub_owned = jnp.sum(hub_parts, axis=0)

    halo_back = transposed_dot(counts_halo, scaled_grads)
    returned = lax.all_to_all(
        halo_back.astype(jnp.bfloat16).reshape(peer_count, slot_count, feature_width),
        "col",
        split_axis=0,
        concat_axis=0,
        tiled=True,
    )
    grad_rows = grad_direct + transposed_dot(counts_own, scaled_grads)
    grad_rows = grad_rows + transposed_dot(picks, returned.reshape(halo_width, feature_width))
    grad_rows = grad_rows.at[hub_rows].add(hub_owned)
    return (output_rows, grad_rows)


def solution(mesh):
    return jax.shard_map(
        local,
        mesh=mesh,
        in_specs=(
            P(("row", "col"), None),
            P(("row", "col"), None),
            P(("row", "col")),
            P(("row", "col")),
            P(("row", "col"), None),
            P(),
            P(),
            P(),
            P(("row", "col"), None),
        ),
        out_specs=(P(("row", "col"), None), P(("row", "col"), None)),
        check_vma=False,
    )
```

```python
import jax
import jax.numpy as jnp
from jax import lax
from jax.sharding import Mesh, PartitionSpec as P


def smooth_gate(values):
    return jax.nn.gelu(values, approximate=True)


def count_matrix(index_rows, start, width):
    degree = index_rows.shape[1]
    narrow_rows = index_rows.astype(jnp.int16)
    column_ids = jnp.arange(start, start + width, dtype=jnp.int16)
    counts = (narrow_rows[:, 0:1] == column_ids[None, :]).astype(jnp.bfloat16)
    for slot in range(1, degree):
        counts = counts + (narrow_rows[:, slot : slot + 1] == column_ids[None, :]).astype(
            jnp.bfloat16
        )
    return counts


def transposed_dot(counts, values):
    return lax.dot_general(
        counts, values, (((0,), (0,)), ((), ())), preferred_element_type=jnp.float32
    )


def local(
    features, send_rows, send_count, hub_rows, neighbours, w_self, w_neigh, bias_vector, cotangent
):
    vertex_count, feature_width = features.shape
    slot_count = send_rows.shape[1]
    degree = neighbours.shape[1]
    peer_count = lax.axis_size("col")
    hub_count = hub_rows.shape[0]
    device_count = lax.axis_size("z") * lax.axis_size("core") * peer_count
    halo_width = peer_count * slot_count
    hub_start = vertex_count + halo_width
    live_mask = jnp.arange(slot_count)[None, :] < send_count[:, None]
    row_ids = jnp.arange(vertex_count, dtype=jnp.int32)
    picks = ((send_rows[:, :, None] == row_ids) & live_mask[:, :, None]).astype(features.dtype)
    picks = picks.reshape(halo_width, vertex_count)
    outgoing = jnp.dot(picks, features, preferred_element_type=jnp.float32).astype(features.dtype)
    outgoing = outgoing.reshape(peer_count, slot_count, feature_width)
    incoming = lax.all_to_all(outgoing, "col", split_axis=0, concat_axis=0, tiled=True)
    incoming = incoming.reshape(-1, feature_width)
    hub_local = features[hub_rows]
    hub_table = lax.all_gather(hub_local, ("z", "core", "col"), axis=0, tiled=True)

    counts_own = count_matrix(neighbours, 0, vertex_count)
    counts_halo = count_matrix(neighbours, vertex_count, halo_width)
    counts_hub = count_matrix(neighbours, hub_start, device_count * hub_count)
    counts_own, counts_halo, counts_hub = lax.optimization_barrier(
        (counts_own, counts_halo, counts_hub)
    )

    summed = jnp.dot(counts_own, features, preferred_element_type=jnp.float32)
    summed = summed + jnp.dot(counts_halo, incoming, preferred_element_type=jnp.float32)
    summed = summed + jnp.dot(counts_hub, hub_table, preferred_element_type=jnp.float32)
    aggregated = (summed * (1.0 / degree)).astype(jnp.bfloat16)
    preact = jnp.dot(features, w_self, preferred_element_type=jnp.float32)
    preact = preact + jnp.dot(aggregated, w_neigh, preferred_element_type=jnp.float32) + bias_vector
    output_rows = smooth_gate(preact).astype(jnp.bfloat16)
    unused, backward = jax.vjp(smooth_gate, preact)
    grad_preact = backward(cotangent.astype(jnp.float32))[0].astype(jnp.bfloat16)
    grad_direct = jnp.dot(grad_preact, w_self.T, preferred_element_type=jnp.float32)
    grad_aggregated = jnp.dot(grad_preact, w_neigh.T, preferred_element_type=jnp.float32).astype(
        jnp.bfloat16
    )
    scaled_grads = (grad_aggregated.astype(jnp.float32) * (1.0 / degree)).astype(jnp.bfloat16)

    hub_back = transposed_dot(counts_hub, scaled_grads)
    core_count = lax.axis_size("core")
    plane_count = device_count // core_count
    hub_pair = lax.all_to_all(
        hub_back.reshape(plane_count // peer_count, core_count, peer_count * hub_count, feature_width),
        "core",
        split_axis=1,
        concat_axis=1,
        tiled=True,
    )
    hub_pair = jnp.sum(hub_pair, axis=1).reshape(plane_count, hub_count, feature_width)
    hub_parts = lax.all_to_all(hub_pair, ("z", "col"), split_axis=0, concat_axis=0, tiled=True)
    hub_owned = jnp.sum(hub_parts, axis=0)

    halo_back = transposed_dot(counts_halo, scaled_grads)
    returned = lax.all_to_all(
        halo_back.astype(jnp.bfloat16).reshape(peer_count, slot_count, feature_width),
        "col",
        split_axis=0,
        concat_axis=0,
        tiled=True,
    )
    grad_rows = grad_direct + transposed_dot(counts_own, scaled_grads)
    grad_rows = grad_rows + transposed_dot(picks, returned.reshape(halo_width, feature_width))
    grad_rows = grad_rows.at[hub_rows].add(hub_owned)
    return (output_rows, grad_rows)


def solution(mesh):
    row_size, col_size = mesh.devices.shape
    split_mesh = Mesh(mesh.devices.reshape(row_size // 2, 2, col_size), ("z", "core", "col"))
    return jax.shard_map(
        local,
        mesh=split_mesh,
        in_specs=(
            P(("z", "core", "col"), None),
            P(("z", "core", "col"), None),
            P(("z", "core", "col")),
            P(("z", "core", "col")),
            P(("z", "core", "col"), None),
            P(),
            P(),
            P(),
            P(("z", "core", "col"), None),
        ),
        out_specs=(P(("z", "core", "col"), None), P(("z", "core", "col"), None)),
        check_vma=False,
    )
```

```python
import jax
import jax.numpy as jnp
from jax import lax
from jax.sharding import PartitionSpec as P


def smooth_gate(values):
    return jax.nn.gelu(values, approximate=True)


def count_matrix(index_rows, start, width):
    degree = index_rows.shape[1]
    narrow_rows = index_rows.astype(jnp.int16)
    column_ids = jnp.arange(start, start + width, dtype=jnp.int16)
    counts = (narrow_rows[:, 0:1] == column_ids[None, :]).astype(jnp.bfloat16)
    for slot in range(1, degree):
        counts = counts + (narrow_rows[:, slot : slot + 1] == column_ids[None, :]).astype(
            jnp.bfloat16
        )
    return counts


def transposed_dot(counts, values):
    return lax.dot_general(
        counts, values, (((0,), (0,)), ((), ())), preferred_element_type=jnp.float32
    )


def local(
    features, send_rows, send_count, hub_rows, neighbours, w_self, w_neigh, bias_vector, cotangent
):
    vertex_count, feature_width = features.shape
    slot_count = send_rows.shape[1]
    degree = neighbours.shape[1]
    peer_count = lax.axis_size("col")
    hub_count = hub_rows.shape[0]
    device_count = lax.axis_size("row") * peer_count
    halo_width = peer_count * slot_count
    hub_start = vertex_count + halo_width
    live_mask = jnp.arange(slot_count)[None, :] < send_count[:, None]
    row_ids = jnp.arange(vertex_count, dtype=jnp.int32)
    picks = ((send_rows[:, :, None] == row_ids) & live_mask[:, :, None]).astype(features.dtype)
    picks = picks.reshape(halo_width, vertex_count)
    outgoing = jnp.dot(picks, features, preferred_element_type=jnp.float32).astype(features.dtype)
    outgoing = outgoing.reshape(peer_count, slot_count, feature_width)
    incoming = lax.all_to_all(outgoing, "col", split_axis=0, concat_axis=0, tiled=True)
    incoming = incoming.reshape(-1, feature_width)
    hub_local = features[hub_rows]
    hub_table = lax.all_gather(hub_local, ("row", "col"), axis=0, tiled=True)

    source_count = hub_start + device_count * hub_count
    piece_count = source_count // vertex_count
    counts = lax.optimization_barrier(
        [count_matrix(neighbours, k * vertex_count, vertex_count) for k in range(piece_count)]
    )
    halo_pieces = halo_width // vertex_count
    counts_own = counts[0]
    counts_halo = counts[1 : 1 + halo_pieces]
    counts_hub = counts[1 + halo_pieces :]
    tables = [features]
    tables += [incoming[k * vertex_count : (k + 1) * vertex_count] for k in range(halo_pieces)]
    tables += [
        hub_table[k * vertex_count : (k + 1) * vertex_count] for k in range(len(counts_hub))
    ]
    summed = jnp.dot(counts[0], tables[0], preferred_element_type=jnp.float32)
    for piece, table in zip(counts[1:], tables[1:]):
        summed = summed + jnp.dot(piece, table, preferred_element_type=jnp.float32)
    aggregated = (summed * (1.0 / degree)).astype(jnp.bfloat16)
    preact = jnp.dot(features, w_self, preferred_element_type=jnp.float32)
    preact = preact + jnp.dot(aggregated, w_neigh, preferred_element_type=jnp.float32) + bias_vector
    output_rows = smooth_gate(preact).astype(jnp.bfloat16)
    unused, backward = jax.vjp(smooth_gate, preact)
    grad_preact = backward(cotangent.astype(jnp.float32))[0].astype(jnp.bfloat16)
    grad_direct = jnp.dot(grad_preact, w_self.T, preferred_element_type=jnp.float32)
    grad_aggregated = jnp.dot(grad_preact, w_neigh.T, preferred_element_type=jnp.float32).astype(
        jnp.bfloat16
    )
    scaled_grads = (grad_aggregated.astype(jnp.float32) * (1.0 / degree)).astype(jnp.bfloat16)

    hub_back = jnp.concatenate([transposed_dot(piece, scaled_grads) for piece in counts_hub], axis=0)
    hub_parts = lax.all_to_all(
        hub_back.reshape(device_count, hub_count, feature_width),
        ("row", "col"),
        split_axis=0,
        concat_axis=0,
        tiled=True,
    )
    hub_owned = jnp.sum(hub_parts, axis=0)

    halo_back = jnp.concatenate([transposed_dot(piece, scaled_grads) for piece in counts_halo], axis=0)
    returned = lax.all_to_all(
        halo_back.astype(jnp.bfloat16).reshape(peer_count, slot_count, feature_width),
        "col",
        split_axis=0,
        concat_axis=0,
        tiled=True,
    )
    grad_rows = grad_direct + transposed_dot(counts_own, scaled_grads)
    grad_rows = grad_rows + transposed_dot(picks, returned.reshape(halo_width, feature_width))
    grad_rows = grad_rows.at[hub_rows].add(hub_owned)
    return (output_rows, grad_rows)


def solution(mesh):
    return jax.shard_map(
        local,
        mesh=mesh,
        in_specs=(
            P(("row", "col"), None),
            P(("row", "col"), None),
            P(("row", "col")),
            P(("row", "col")),
            P(("row", "col"), None),
            P(),
            P(),
            P(),
            P(("row", "col"), None),
        ),
        out_specs=(P(("row", "col"), None), P(("row", "col"), None)),
        check_vma=False,
    )
```

```python
import jax
import jax.numpy as jnp
from jax import lax
from jax.sharding import PartitionSpec as P


def smooth_gate(values):
    return jax.nn.gelu(values, approximate=True)


def count_matrix(index_rows, start, width):
    degree = index_rows.shape[1]
    narrow_rows = index_rows.astype(jnp.int16)
    column_ids = jnp.arange(start, start + width, dtype=jnp.int16)
    counts = (narrow_rows[:, 0:1] == column_ids[None, :]).astype(jnp.bfloat16)
    for slot in range(1, degree):
        counts = counts + (narrow_rows[:, slot : slot + 1] == column_ids[None, :]).astype(
            jnp.bfloat16
        )
    return counts


def transposed_dot(counts, values):
    return lax.dot_general(
        counts, values, (((0,), (0,)), ((), ())), preferred_element_type=jnp.float32
    )


def local(
    features, send_rows, send_count, hub_rows, neighbours, w_self, w_neigh, bias_vector, cotangent
):
    vertex_count, feature_width = features.shape
    slot_count = send_rows.shape[1]
    degree = neighbours.shape[1]
    peer_count = lax.axis_size("col")
    hub_count = hub_rows.shape[0]
    device_count = lax.axis_size("row") * peer_count
    halo_width = peer_count * slot_count
    hub_start = vertex_count + halo_width
    live_mask = jnp.arange(slot_count)[None, :] < send_count[:, None]
    row_ids = jnp.arange(vertex_count, dtype=jnp.int32)
    picks = ((send_rows[:, :, None] == row_ids) & live_mask[:, :, None]).astype(features.dtype)
    picks = picks.reshape(halo_width, vertex_count)
    outgoing = jnp.dot(picks, features, preferred_element_type=jnp.float32).astype(features.dtype)
    outgoing = outgoing.reshape(peer_count, slot_count, feature_width)
    incoming = lax.all_to_all(outgoing, "col", split_axis=0, concat_axis=0, tiled=True)
    incoming = incoming.reshape(-1, feature_width)
    hub_local = features[hub_rows]
    hub_copies = jnp.broadcast_to(hub_local[None], (device_count, hub_count, feature_width))
    hub_table = lax.all_to_all(hub_copies, ("row", "col"), split_axis=0, concat_axis=0, tiled=True)
    hub_table = hub_table.reshape(device_count * hub_count, feature_width)

    counts_own = count_matrix(neighbours, 0, vertex_count)
    counts_halo = count_matrix(neighbours, vertex_count, halo_width)
    counts_hub = count_matrix(neighbours, hub_start, device_count * hub_count)
    counts_own, counts_halo, counts_hub = lax.optimization_barrier(
        (counts_own, counts_halo, counts_hub)
    )

    summed = jnp.dot(counts_own, features, preferred_element_type=jnp.float32)
    summed = summed + jnp.dot(counts_halo, incoming, preferred_element_type=jnp.float32)
    summed = summed + jnp.dot(counts_hub, hub_table, preferred_element_type=jnp.float32)
    aggregated = (summed * (1.0 / degree)).astype(jnp.bfloat16)
    preact = jnp.dot(features, w_self, preferred_element_type=jnp.float32)
    preact = preact + jnp.dot(aggregated, w_neigh, preferred_element_type=jnp.float32) + bias_vector
    output_rows = smooth_gate(preact).astype(jnp.bfloat16)
    unused, backward = jax.vjp(smooth_gate, preact)
    grad_preact = backward(cotangent.astype(jnp.float32))[0].astype(jnp.bfloat16)
    grad_direct = jnp.dot(grad_preact, w_self.T, preferred_element_type=jnp.float32)
    grad_aggregated = jnp.dot(grad_preact, w_neigh.T, preferred_element_type=jnp.float32).astype(
        jnp.bfloat16
    )
    scaled_grads = (grad_aggregated.astype(jnp.float32) * (1.0 / degree)).astype(jnp.bfloat16)

    hub_back = transposed_dot(counts_hub, scaled_grads)
    hub_parts = lax.all_to_all(
        hub_back.reshape(device_count, hub_count, feature_width),
        ("row", "col"),
        split_axis=0,
        concat_axis=0,
        tiled=True,
    )
    hub_owned = jnp.sum(hub_parts, axis=0)

    halo_back = transposed_dot(counts_halo, scaled_grads)
    returned = lax.all_to_all(
        halo_back.astype(jnp.bfloat16).reshape(peer_count, slot_count, feature_width),
        "col",
        split_axis=0,
        concat_axis=0,
        tiled=True,
    )
    grad_rows = grad_direct + transposed_dot(counts_own, scaled_grads)
    grad_rows = grad_rows + transposed_dot(picks, returned.reshape(halo_width, feature_width))
    grad_rows = grad_rows.at[hub_rows].add(hub_owned)
    return (output_rows, grad_rows)


def solution(mesh):
    return jax.shard_map(
        local,
        mesh=mesh,
        in_specs=(
            P(("row", "col"), None),
            P(("row", "col"), None),
            P(("row", "col")),
            P(("row", "col")),
            P(("row", "col"), None),
            P(),
            P(),
            P(),
            P(("row", "col"), None),
        ),
        out_specs=(P(("row", "col"), None), P(("row", "col"), None)),
        check_vma=False,
    )
```

```python
import jax
import jax.numpy as jnp
from jax import lax
from jax.sharding import PartitionSpec as P


def smooth_gate(values):
    return jax.nn.gelu(values, approximate=True)


def count_matrix(index_rows, start, width):
    degree = index_rows.shape[1]
    narrow_rows = index_rows.astype(jnp.int16)
    column_ids = jnp.arange(start, start + width, dtype=jnp.int16)
    counts = (narrow_rows[:, 0:1] == column_ids[None, :]).astype(jnp.bfloat16)
    for slot in range(1, degree):
        counts = counts + (narrow_rows[:, slot : slot + 1] == column_ids[None, :]).astype(
            jnp.bfloat16
        )
    return counts


def transposed_dot(counts, values):
    return lax.dot_general(
        counts, values, (((0,), (0,)), ((), ())), preferred_element_type=jnp.float32
    )


def local(
    features, send_rows, send_count, hub_rows, neighbours, w_self, w_neigh, bias_vector, cotangent
):
    vertex_count, feature_width = features.shape
    slot_count = send_rows.shape[1]
    degree = neighbours.shape[1]
    peer_count = lax.axis_size("col")
    hub_count = hub_rows.shape[0]
    device_count = lax.axis_size("row") * peer_count
    halo_width = peer_count * slot_count
    hub_start = vertex_count + halo_width
    live_mask = jnp.arange(slot_count)[None, :] < send_count[:, None]
    row_ids = jnp.arange(vertex_count, dtype=jnp.int32)
    picks = ((send_rows[:, :, None] == row_ids) & live_mask[:, :, None]).astype(features.dtype)
    picks = picks.reshape(halo_width, vertex_count)
    outgoing = jnp.dot(picks, features, preferred_element_type=jnp.float32).astype(features.dtype)
    outgoing = outgoing.reshape(peer_count, slot_count, feature_width)
    hub_local = features[hub_rows]
    hub_copies = jnp.broadcast_to(hub_local[None], (peer_count, hub_count, feature_width))
    outgoing = jnp.concatenate([outgoing, hub_copies], axis=1)
    arrived = lax.all_to_all(outgoing, "col", split_axis=0, concat_axis=0, tiled=True)
    incoming = arrived[:, :slot_count].reshape(-1, feature_width)
    hub_row_part = arrived[:, slot_count:].reshape(peer_count * hub_count, feature_width)
    row_count = device_count // peer_count
    hub_copies = jnp.broadcast_to(hub_row_part[None], (row_count,) + hub_row_part.shape)
    hub_table = lax.all_to_all(hub_copies, "row", split_axis=0, concat_axis=0, tiled=True)
    hub_table = hub_table.reshape(device_count * hub_count, feature_width)

    counts_own = count_matrix(neighbours, 0, vertex_count)
    counts_halo = count_matrix(neighbours, vertex_count, halo_width)
    counts_hub = count_matrix(neighbours, hub_start, device_count * hub_count)
    counts_own, counts_halo, counts_hub = lax.optimization_barrier(
        (counts_own, counts_halo, counts_hub)
    )

    summed = jnp.dot(counts_own, features, preferred_element_type=jnp.float32)
    summed = summed + jnp.dot(counts_halo, incoming, preferred_element_type=jnp.float32)
    summed = summed + jnp.dot(counts_hub, hub_table, preferred_element_type=jnp.float32)
    aggregated = (summed * (1.0 / degree)).astype(jnp.bfloat16)
    preact = jnp.dot(features, w_self, preferred_element_type=jnp.float32)
    preact = preact + jnp.dot(aggregated, w_neigh, preferred_element_type=jnp.float32) + bias_vector
    output_rows = smooth_gate(preact).astype(jnp.bfloat16)
    unused, backward = jax.vjp(smooth_gate, preact)
    grad_preact = backward(cotangent.astype(jnp.float32))[0].astype(jnp.bfloat16)
    grad_direct = jnp.dot(grad_preact, w_self.T, preferred_element_type=jnp.float32)
    grad_aggregated = jnp.dot(grad_preact, w_neigh.T, preferred_element_type=jnp.float32).astype(
        jnp.bfloat16
    )
    scaled_grads = (grad_aggregated.astype(jnp.float32) * (1.0 / degree)).astype(jnp.bfloat16)

    hub_back = transposed_dot(counts_hub, scaled_grads)
    hub_parts = lax.all_to_all(
        hub_back.reshape(device_count, hub_count, feature_width),
        ("row", "col"),
        split_axis=0,
        concat_axis=0,
        tiled=True,
    )
    hub_owned = jnp.sum(hub_parts, axis=0)

    halo_back = transposed_dot(counts_halo, scaled_grads)
    returned = lax.all_to_all(
        halo_back.astype(jnp.bfloat16).reshape(peer_count, slot_count, feature_width),
        "col",
        split_axis=0,
        concat_axis=0,
        tiled=True,
    )
    grad_rows = grad_direct + transposed_dot(counts_own, scaled_grads)
    grad_rows = grad_rows + transposed_dot(picks, returned.reshape(halo_width, feature_width))
    grad_rows = grad_rows.at[hub_rows].add(hub_owned)
    return (output_rows, grad_rows)


def solution(mesh):
    return jax.shard_map(
        local,
        mesh=mesh,
        in_specs=(
            P(("row", "col"), None),
            P(("row", "col"), None),
            P(("row", "col")),
            P(("row", "col")),
            P(("row", "col"), None),
            P(),
            P(),
            P(),
            P(("row", "col"), None),
        ),
        out_specs=(P(("row", "col"), None), P(("row", "col"), None)),
        check_vma=False,
    )
```

```python
import jax
import jax.numpy as jnp
from jax import lax
from jax.sharding import PartitionSpec as P


def smooth_gate(values):
    return jax.nn.gelu(values, approximate=True)


def count_matrix(index_rows, start, width):
    degree = index_rows.shape[1]
    narrow_rows = index_rows.astype(jnp.int16)
    column_ids = jnp.arange(start, start + width, dtype=jnp.int16)
    counts = (narrow_rows[:, 0:1] == column_ids[None, :]).astype(jnp.bfloat16)
    for slot in range(1, degree):
        counts = counts + (narrow_rows[:, slot : slot + 1] == column_ids[None, :]).astype(
            jnp.bfloat16
        )
    return counts


def transposed_dot(counts, values):
    return lax.dot_general(
        counts, values, (((0,), (0,)), ((), ())), preferred_element_type=jnp.float32
    )


def local(
    features, send_rows, send_count, hub_rows, neighbours, w_self, w_neigh, bias_vector, cotangent
):
    vertex_count, feature_width = features.shape
    slot_count = send_rows.shape[1]
    degree = neighbours.shape[1]
    peer_count = lax.axis_size("col")
    hub_count = hub_rows.shape[0]
    device_count = lax.axis_size("row") * peer_count
    halo_width = peer_count * slot_count
    hub_start = vertex_count + halo_width
    live_mask = jnp.arange(slot_count)[None, :] < send_count[:, None]
    row_ids = jnp.arange(vertex_count, dtype=jnp.int32)
    picks = ((send_rows[:, :, None] == row_ids) & live_mask[:, :, None]).astype(features.dtype)
    picks = picks.reshape(halo_width, vertex_count)
    outgoing = jnp.dot(picks, features, preferred_element_type=jnp.float32).astype(features.dtype)
    outgoing = outgoing.reshape(peer_count, slot_count, feature_width)
    hub_local = features[hub_rows]
    hub_copies = jnp.broadcast_to(hub_local[None], (peer_count, hub_count, feature_width))
    outgoing = jnp.concatenate([outgoing, hub_copies], axis=1)
    arrived = lax.all_to_all(outgoing, "col", split_axis=0, concat_axis=0, tiled=True)
    incoming = arrived[:, :slot_count].reshape(-1, feature_width)
    hub_row_part = arrived[:, slot_count:].reshape(peer_count * hub_count, feature_width)
    row_count = device_count // peer_count
    hub_copies = jnp.broadcast_to(hub_row_part[None], (row_count,) + hub_row_part.shape)
    hub_table = lax.all_to_all(hub_copies, "row", split_axis=0, concat_axis=0, tiled=True)
    hub_table = hub_table.reshape(device_count * hub_count, feature_width)

    source_table = jnp.concatenate([features, incoming, hub_table], axis=0)
    half = source_table.shape[0] // 2
    counts_low = count_matrix(neighbours, 0, half)
    counts_high = count_matrix(neighbours, half, half)
    counts_low, counts_high = lax.optimization_barrier((counts_low, counts_high))

    summed = jnp.dot(counts_low, source_table[:half], preferred_element_type=jnp.float32)
    summed = summed + jnp.dot(counts_high, source_table[half:], preferred_element_type=jnp.float32)
    aggregated = (summed * (1.0 / degree)).astype(jnp.bfloat16)
    preact = jnp.dot(features, w_self, preferred_element_type=jnp.float32)
    preact = preact + jnp.dot(aggregated, w_neigh, preferred_element_type=jnp.float32) + bias_vector
    output_rows = smooth_gate(preact).astype(jnp.bfloat16)
    unused, backward = jax.vjp(smooth_gate, preact)
    grad_preact = backward(cotangent.astype(jnp.float32))[0].astype(jnp.bfloat16)
    grad_direct = jnp.dot(grad_preact, w_self.T, preferred_element_type=jnp.float32)
    grad_aggregated = jnp.dot(grad_preact, w_neigh.T, preferred_element_type=jnp.float32).astype(
        jnp.bfloat16
    )
    scaled_grads = (grad_aggregated.astype(jnp.float32) * (1.0 / degree)).astype(jnp.bfloat16)

    back_low = transposed_dot(counts_low, scaled_grads)
    back_high = transposed_dot(counts_high, scaled_grads)
    table_grads = jnp.concatenate([back_low, back_high], axis=0)
    hub_back = table_grads[hub_start:]
    hub_parts = lax.all_to_all(
        hub_back.reshape(device_count, hub_count, feature_width),
        ("row", "col"),
        split_axis=0,
        concat_axis=0,
        tiled=True,
    )
    hub_owned = jnp.sum(hub_parts, axis=0)

    halo_back = table_grads[vertex_count:hub_start]
    returned = lax.all_to_all(
        halo_back.astype(jnp.bfloat16).reshape(peer_count, slot_count, feature_width),
        "col",
        split_axis=0,
        concat_axis=0,
        tiled=True,
    )
    grad_rows = grad_direct + table_grads[:vertex_count]
    grad_rows = grad_rows + transposed_dot(picks, returned.reshape(halo_width, feature_width))
    grad_rows = grad_rows.at[hub_rows].add(hub_owned)
    return (output_rows, grad_rows)


def solution(mesh):
    return jax.shard_map(
        local,
        mesh=mesh,
        in_specs=(
            P(("row", "col"), None),
            P(("row", "col"), None),
            P(("row", "col")),
            P(("row", "col")),
            P(("row", "col"), None),
            P(),
            P(),
            P(),
            P(("row", "col"), None),
        ),
        out_specs=(P(("row", "col"), None), P(("row", "col"), None)),
        check_vma=False,
    )
```

```python
import jax
import jax.numpy as jnp
from jax import lax
from jax.sharding import PartitionSpec as P


def smooth_gate(values):
    return jax.nn.gelu(values, approximate=True)


def count_matrix(index_rows, start, width):
    degree = index_rows.shape[1]
    narrow_rows = index_rows.astype(jnp.int16)
    column_ids = jnp.arange(start, start + width, dtype=jnp.int16)
    counts = (narrow_rows[:, 0:1] == column_ids[None, :]).astype(jnp.bfloat16)
    for slot in range(1, degree):
        counts = counts + (narrow_rows[:, slot : slot + 1] == column_ids[None, :]).astype(
            jnp.bfloat16
        )
    return counts


def transposed_dot(counts, values):
    return lax.dot_general(
        counts, values, (((0,), (0,)), ((), ())), preferred_element_type=jnp.float32
    )


def local(
    features, send_rows, send_count, hub_rows, neighbours, w_self, w_neigh, bias_vector, cotangent
):
    vertex_count, feature_width = features.shape
    slot_count = send_rows.shape[1]
    degree = neighbours.shape[1]
    peer_count = lax.axis_size("col")
    hub_count = hub_rows.shape[0]
    device_count = lax.axis_size("row") * peer_count
    halo_width = peer_count * slot_count
    hub_start = vertex_count + halo_width
    live_mask = jnp.arange(slot_count)[None, :] < send_count[:, None]
    row_ids = jnp.arange(vertex_count, dtype=jnp.int16)
    narrow_sends = jnp.where(live_mask, send_rows, -1).astype(jnp.int16)
    picks = (narrow_sends[:, :, None] == row_ids).astype(features.dtype)
    picks = picks.reshape(halo_width, vertex_count)
    outgoing = jnp.dot(picks, features, preferred_element_type=jnp.float32).astype(features.dtype)
    outgoing = outgoing.reshape(peer_count, slot_count, feature_width)
    hub_local = features[hub_rows]
    hub_copies = jnp.broadcast_to(hub_local[None], (peer_count, hub_count, feature_width))
    outgoing = jnp.concatenate([outgoing, hub_copies], axis=1)
    arrived = lax.all_to_all(outgoing, "col", split_axis=0, concat_axis=0, tiled=True)
    incoming = arrived[:, :slot_count].reshape(-1, feature_width)
    hub_row_part = arrived[:, slot_count:].reshape(peer_count * hub_count, feature_width)
    row_count = device_count // peer_count
    hub_copies = jnp.broadcast_to(hub_row_part[None], (row_count,) + hub_row_part.shape)
    hub_table = lax.all_to_all(hub_copies, "row", split_axis=0, concat_axis=0, tiled=True)
    hub_table = hub_table.reshape(device_count * hub_count, feature_width)

    counts_own = count_matrix(neighbours, 0, vertex_count)
    counts_halo = count_matrix(neighbours, vertex_count, halo_width)
    counts_hub = count_matrix(neighbours, hub_start, device_count * hub_count)
    counts_own, counts_halo, counts_hub = lax.optimization_barrier(
        (counts_own, counts_halo, counts_hub)
    )

    summed = jnp.dot(counts_own, features, preferred_element_type=jnp.float32)
    summed = summed + jnp.dot(counts_halo, incoming, preferred_element_type=jnp.float32)
    summed = summed + jnp.dot(counts_hub, hub_table, preferred_element_type=jnp.float32)
    aggregated = (summed * (1.0 / degree)).astype(jnp.bfloat16)
    preact = jnp.dot(features, w_self, preferred_element_type=jnp.float32)
    preact = preact + jnp.dot(aggregated, w_neigh, preferred_element_type=jnp.float32) + bias_vector
    output_rows = smooth_gate(preact).astype(jnp.bfloat16)
    unused, backward = jax.vjp(smooth_gate, preact)
    grad_preact = backward(cotangent.astype(jnp.float32))[0].astype(jnp.bfloat16)
    grad_direct = jnp.dot(grad_preact, w_self.T, preferred_element_type=jnp.float32)
    grad_aggregated = jnp.dot(grad_preact, w_neigh.T, preferred_element_type=jnp.float32).astype(
        jnp.bfloat16
    )
    scaled_grads = (grad_aggregated.astype(jnp.float32) * (1.0 / degree)).astype(jnp.bfloat16)

    hub_back = transposed_dot(counts_hub, scaled_grads)
    hub_parts = lax.all_to_all(
        hub_back.reshape(device_count, hub_count, feature_width),
        ("row", "col"),
        split_axis=0,
        concat_axis=0,
        tiled=True,
    )
    hub_owned = jnp.sum(hub_parts, axis=0)

    halo_back = transposed_dot(counts_halo, scaled_grads)
    returned = lax.all_to_all(
        halo_back.astype(jnp.bfloat16).reshape(peer_count, slot_count, feature_width),
        "col",
        split_axis=0,
        concat_axis=0,
        tiled=True,
    )
    grad_rows = grad_direct + transposed_dot(counts_own, scaled_grads)
    grad_rows = grad_rows + transposed_dot(picks, returned.reshape(halo_width, feature_width))
    grad_rows = grad_rows.at[hub_rows].add(hub_owned)
    return (output_rows, grad_rows)


def solution(mesh):
    return jax.shard_map(
        local,
        mesh=mesh,
        in_specs=(
            P(("row", "col"), None),
            P(("row", "col"), None),
            P(("row", "col")),
            P(("row", "col")),
            P(("row", "col"), None),
            P(),
            P(),
            P(),
            P(("row", "col"), None),
        ),
        out_specs=(P(("row", "col"), None), P(("row", "col"), None)),
        check_vma=False,
    )
```
